32 devices in a mesh: blk: 16 (over z, y, core), rep: 2 (over x).
Axes of the slice: x: 2, y: 2, z: 4, core: 2. Of those that a mesh axis runs over, the one named last changes fastest.
Arguments:
- grad_out: bfloat16 [24576, 256], P('blk'), may hold values from -6 to 6
- pre_act: bfloat16 [24576, 256], P('blk'), may hold values from -6 to 6
- prev_pre: bfloat16 [24576, 256], P(('blk', 'rep')), may hold values from -6 to 6
- weight: bfloat16 [256, 256], replicated, may hold values from -0.375 to 0.375
- block_values: bfloat16 [3840, 128, 128], P(('blk', 'rep')), may hold values from -0.25 to 0.25
- block_rows: int32 [3840], P(('blk', 'rep')), may hold values from 0 to 11, as said below
- block_cols: int32 [3840], P(('blk', 'rep')), may hold values from 0 to 59
Outputs:
- grad_in: bfloat16 [24576, 256], P(('blk', 'rep'))
- grad_weight: float32 [256, 256], replicated
The draws below stay inside these ranges and needn't reach their ends.
Inputs may be any that keep to these rules, and one draw needn't show every extreme that they name: The blocks of the 2 devices of one stripe sit at distinct (block_rows, block_cols) positions.
All inputs are finite; a program needn't handle non-finite values.
Results may differ from the reference program's by a relative error of at most 0.0049.
Values sent between devices are 32-bit elements; how exact they have to be, the bound alone decides.
A program may use at most 192 MiB of HBM per device.

```python
import math
import jax
import jax.numpy as jnp
from jax import lax

F = 256
BS = 128
HALO = 2
ROWB = 6
BPD = 120
SB = 12
NODES = 24576
BLKS = 3840
N_REP = 2
DEVICES = 32


def stripe_positions(key):
    per_stripe = BPD * N_REP
    stripes = BLKS // per_stripe
    spots = (2 * HALO + 1) * SB * SB
    base = jax.random.fold_in(key, 7071)

    def one_stripe(index):
        order = jax.random.permutation(jax.random.fold_in(base, index), spots)
        return order[:per_stripe].astype(jnp.int32)
    chosen = jax.vmap(one_stripe)(jnp.arange(stripes, dtype=jnp.int32))
    return chosen.reshape(BLKS)


def draw_block_rows(key, part):
    chosen = stripe_positions(key)
    return (chosen // ((2 * HALO + 1) * SB)).astype(jnp.int32)


def draw_block_cols(key, part):
    chosen = stripe_positions(key)
    return (chosen % ((2 * HALO + 1) * SB)).astype(jnp.int32)


def block_scale(own_key, extent, pieces, least, high):
    level, own = 1.0, jax.random.fold_in(own_key, 6)
    for dim, parts in pieces:
        steps = jnp.exp(jax.random.uniform(jax.random.fold_in(own, dim), (parts,), jnp.float32, least / len(pieces), high / len(pieces)))
        level = level * jnp.repeat(steps, extent[dim] // parts).reshape([-1 if axis == dim else 1 for axis in range(len(extent))])
    return level


def normal_values(rng, shape, width, most, cuts=(), held_as=jnp.bfloat16):
    drawn = width * jax.random.normal(rng, shape, jnp.float32)
    if cuts:
        drawn = drawn * block_scale(rng, shape, cuts, -0.22, 0.18)
    return jnp.clip(drawn, -most, most).astype(held_as)


def setup_inputs(seed: int = 0) -> dict:
    arg_keys = jax.random.split(jax.random.key(seed), 8)
    grad_out = normal_values(arg_keys[0], (NODES, F), 1.0, 6.0, ((0, 16),))
    pre_act = normal_values(arg_keys[1], (NODES, F), 1.0, 6.0, ((0, 16),))
    prev_pre = normal_values(arg_keys[2], (NODES, F), 1.0, 6.0, ((0, 32),))
    weight = normal_values(arg_keys[3], (F, F), F ** -0.5, 0.375)
    block_values = normal_values(arg_keys[4], (BLKS, BS, BS), (BPD * BS // (5 * ROWB)) ** -0.5, 0.25, ((0, 32),))
    block_rows = draw_block_rows(jax.random.fold_in(arg_keys[7], 71), 0)
    block_cols = draw_block_cols(jax.random.fold_in(arg_keys[7], 71), 0)
    return {"grad_out": grad_out, "pre_act": pre_act, "prev_pre": prev_pre, "weight": weight, "block_values": block_values, "block_rows": block_rows, "block_cols": block_cols}


def reference(grad_out, pre_act, prev_pre, weight, block_values, block_rows, block_cols):
    nblocks = NODES // BS
    masked = grad_out * (pre_act > 0).astype(jnp.bfloat16)
    masked_blocks = masked.reshape(nblocks, BS, F)
    holder = jnp.arange(BLKS, dtype=jnp.int32) // BPD
    stripe = holder // N_REP
    global_rows = (stripe * SB + block_rows).astype(jnp.int32)
    global_cols = jnp.mod((stripe - HALO) * SB + block_cols, nblocks).astype(jnp.int32)
    values_grouped = block_values.reshape(DEVICES, BPD, BS, BS)
    rows_grouped = global_rows.reshape(DEVICES, BPD)
    cols_grouped = global_cols.reshape(DEVICES, BPD)

    def accumulate(carry, group):
        values, rows, cols = group
        picked = masked_blocks[rows]
        tiles = jnp.einsum('kab,kaf->kbf', values.astype(jnp.float32), picked.astype(jnp.float32))
        return (carry.at[cols].add(tiles), None)
    start = jnp.zeros((nblocks, BS, F), jnp.float32)
    summed, _ = lax.scan(accumulate, start, (values_grouped, rows_grouped, cols_grouped))
    dy16 = summed.reshape(NODES, F).astype(jnp.bfloat16)
    feats = jnp.maximum(prev_pre, jnp.zeros_like(prev_pre))
    grad_weight = jnp.dot(feats.T, dy16, preferred_element_type=jnp.float32) * (1.0 / math.sqrt(NODES))
    grad_in = (jnp.dot(dy16, weight.T, preferred_element_type=jnp.float32) * (prev_pre > 0).astype(jnp.float32)).astype(jnp.bfloat16)
    return (grad_in, grad_weight)
```

```python
import functools
import math

import jax
import jax.numpy as jnp
from jax import lax
from jax.experimental import pallas as pl
from jax.experimental.pallas import tpu as pltpu
from jax.sharding import PartitionSpec as P

HALO = 2
SPANS = 2 * HALO + 1
MESH = pl.DeviceIdType.MESH
VMEM_MAX = 67_043_328
CHUNKS = 8
GROUP = 4
STEP = 24


def window_kernel(rows_ref, cols_ref, grad_ref, pre_ref, values_ref, out_ref, masked, window, sem):
    step = pl.program_id(0)

    @pl.when(step == 0)
    def _():
        masked[...] = jnp.where(pre_ref[...] > 0, grad_ref[...], jnp.zeros_like(grad_ref[...])).reshape(masked.shape)

        @pl.loop(0, window.shape[0])
        def _(i):
            window[i] = jnp.zeros(window.shape[1:], window.dtype)

    count = values_ref.shape[0]

    @pl.loop(0, count // GROUP)
    def _(group):
        tiles = []
        for i in range(GROUP):
            k = group * GROUP + i
            tiles.append(
                lax.dot_general(
                    values_ref[k],
                    masked[rows_ref[step * count + k]],
                    (((0,), (0,)), ((), ())),
                    preferred_element_type=jnp.float32,
                )
            )
        for i in range(GROUP):
            col = cols_ref[step * count + group * GROUP + i]
            window[col] = window[col] + tiles[i]

    @pl.when(step == pl.num_programs(0) - 1)
    def _():
        copy = pltpu.make_async_copy(window, out_ref, sem)
        copy.start()
        copy.wait()


def window_sums(rows, cols, grad_out, pre_act, values):
    count, block, _ = values.shape
    stripe_rows, width = grad_out.shape
    stripe_blocks = stripe_rows // block
    whole = pl.BlockSpec((stripe_rows, width), lambda i, *_: (0, 0))
    return pl.pallas_call(
        window_kernel,
        out_shape=jax.ShapeDtypeStruct((SPANS * stripe_blocks, block, width), jnp.float32),
        grid_spec=pltpu.PrefetchScalarGridSpec(
            num_scalar_prefetch=2,
            grid=(count // STEP,),
            in_specs=[whole, whole, pl.BlockSpec((STEP, block, block), lambda i, *_: (i, 0, 0))],
            out_specs=pl.BlockSpec(memory_space=pl.ANY),
            scratch_shapes=[
                pltpu.VMEM((stripe_blocks, block, width), jnp.bfloat16),
                pltpu.VMEM((SPANS * stripe_blocks, block, width), jnp.float32),
                pltpu.SemaphoreType.DMA,
            ],
        ),
        compiler_params=pltpu.CompilerParams(vmem_limit_bytes=56 << 20),
        name="window_sums",
    )(rows, cols, grad_out, pre_act, values)


def exchange_kernel(
    nb, nr, scale,
    win, prev_ref, weight_ref, grad_in_ref, gw_ref,
    acc, core_in, z_in, y_in, x_in, dy, term, term_in, rep_in, total,
    s_load, s_core, r_core, s_z, r_z, s_y, r_y, s_x, r_x, s_t, r_t, s_r, r_r, s_g, r_g,
):
    b, r = lax.axis_index("blk"), lax.axis_index("rep")
    core, chip = b % 2, b // 2
    y, chips = chip % 2, nb // 2
    rows = dy.shape[0]
    size = rows // CHUNKS

    loads = [pltpu.make_async_copy(win.at[2 * i], acc.at[i], s_load.at[i]) for i in range(3)]
    for load in loads:
        load.start()

    barrier = pltpu.get_barrier_semaphore()
    for d in range(1, nb):
        pl.semaphore_signal(barrier, inc=1, device_id=((b + d) % nb, r), device_id_type=MESH)
    for e in range(1, nr):
        pl.semaphore_signal(barrier, inc=1, device_id=(b, (r + e) % nr), device_id_type=MESH)
    pl.semaphore_wait(barrier, nb - 1 + nr - 1)

    def remote(src, dst, send, recv, to_b, to_r):
        return pltpu.make_async_remote_copy(
            src_ref=src, dst_ref=dst, send_sem=send, recv_sem=recv,
            device_id=(to_b, to_r), device_id_type=MESH,
        )

    def part(j):
        return pl.ds(j * size, size)

    far, near = 2 * y, 2 - 2 * y
    core_to = chip * 2 + 1 - core
    z_to = ((chip + 4 * y - 2 + chips) % chips) * 2 + core
    y_to = (chip + 1 - 2 * y) * 2 + core

    def core_copy(i, j):
        return remote(
            win.at[2 * i + 1, :, part(j), :], core_in.at[i, :, part(j), :],
            s_core.at[i, j], r_core.at[i, j], core_to, r,
        )

    def z_copy(j):
        return remote(acc.at[far, :, part(j), :], z_in.at[:, part(j), :], s_z.at[j], r_z.at[j], z_to, r)

    def y_copy(j):
        return remote(acc.at[near, :, part(j), :], y_in.at[:, part(j), :], s_y.at[j], r_y.at[j], y_to, r)

    def x_copy(e, j):
        q = (r + e) % nr
        return remote(acc.at[1, q, part(j), :], x_in.at[e, part(j), :], s_x.at[e, j], r_x.at[e, j], b, q)

    for j in range(CHUNKS):
        for i in range(2):
            core_copy(i, j).start()
    for load in loads:
        load.wait()

    for j in range(CHUNKS):
        for i in range(2):
            core_copy(i, j).wait_recv()
            acc[1 + i - core, :, part(j), :] += core_in[i, :, part(j), :]
        z_copy(j).start()

    for step in range(CHUNKS + 3):
        if step < CHUNKS:
            j = step
            z_copy(j).wait_recv()
            acc[near, :, part(j), :] += z_in[:, part(j), :]
            y_copy(j).start()
        if 0 <= step - 1 < CHUNKS:
            j = step - 1
            y_copy(j).wait_recv()
            acc[1, :, part(j), :] += y_in[:, part(j), :]
            for e in range(1, nr):
                x_copy(e, j).start()
        if 0 <= step - 3 < CHUNKS:
            j = step - 3
            mine = acc[1, r, part(j), :]
            for e in range(1, nr):
                x_copy(e, j).wait_recv()
                mine = mine + x_in[e, part(j), :]
            dy[part(j), :] = mine.astype(jnp.bfloat16)

    prev = prev_ref[...]
    feats = jnp.maximum(prev, jnp.zeros_like(prev))
    product = lax.dot_general(feats, dy[...], (((0,), (0,)), ((), ())), preferred_element_type=jnp.float32)
    term[...] = product.reshape(term.shape)

    def term_copy(d):
        to = (b + d) % nb
        return remote(term.at[to], term_in.at[d], s_t.at[d], r_t.at[d], to, r)

    def rep_copy(e):
        return remote(rep_in.at[r], rep_in.at[r], s_r.at[e], r_r.at[e], b, (r + e) % nr)

    def total_copy(d):
        return remote(total.at[b], total.at[b], s_g.at[d], r_g.at[d], (b + d) % nb, r)

    for d in range(1, nb):
        term_copy(d).start()
    back = lax.dot_general(dy[...], weight_ref[...], (((1,), (1,)), ((), ())), preferred_element_type=jnp.float32)
    grad_in_ref[...] = jnp.where(prev > 0, back, jnp.zeros_like(back)).astype(jnp.bfloat16)
    own = term[b]
    for d in range(1, nb):
        term_copy(d).wait_recv()
        own = own + term_in[d]
    rep_in[r] = own
    for e in range(1, nr):
        rep_copy(e).start()
    for e in range(1, nr):
        rep_copy(e).wait_recv()
    full = rep_in[0]
    for e in range(1, nr):
        full = full + rep_in[e]
    total[b] = full * scale
    for d in range(1, nb):
        total_copy(d).start()
    for d in range(1, nb):
        total_copy(d).wait_recv()
    gw_ref[...] = total[...].reshape(gw_ref.shape)

    for j in range(CHUNKS):
        for i in range(2):
            core_copy(i, j).wait_send()
        z_copy(j).wait_send()
        y_copy(j).wait_send()
        for e in range(1, nr):
            x_copy(e, j).wait_send()
    for d in range(1, nb):
        term_copy(d).wait_send()
        total_copy(d).wait_send()
    for e in range(1, nr):
        rep_copy(e).wait_send()


def exchange(nb, nr, window, prev_pre, weight, nodes):
    rows, width = prev_pre.shape
    slab = (nr, rows, width)
    f32 = jnp.float32
    piece = (width // nb, width)
    need = 4 * width * rows * (7 * nr + nr + 2) + 12 * 4 * width * width
    dma = pltpu.SemaphoreType.DMA
    vmem = pl.BlockSpec(memory_space=pltpu.VMEM)
    return pl.pallas_call(
        functools.partial(exchange_kernel, nb, nr, 1.0 / math.sqrt(nodes)),
        out_shape=(
            jax.ShapeDtypeStruct((rows, width), jnp.bfloat16),
            jax.ShapeDtypeStruct((width, width), f32),
        ),
        in_specs=[pl.BlockSpec(memory_space=pl.ANY), vmem, vmem],
        out_specs=(vmem, vmem),
        scratch_shapes=[
            pltpu.VMEM((3,) + slab, f32),
            pltpu.VMEM((2,) + slab, f32),
            pltpu.VMEM(slab, f32),
            pltpu.VMEM(slab, f32),
            pltpu.VMEM(slab, f32),
            pltpu.VMEM((rows, width), jnp.bfloat16),
            pltpu.VMEM((nb,) + piece, f32),
            pltpu.VMEM((nb,) + piece, f32),
            pltpu.VMEM((nr,) + piece, f32),
            pltpu.VMEM((nb,) + piece, f32),
            dma((3,)),
            dma((2, CHUNKS)), dma((2, CHUNKS)),
            dma((CHUNKS,)), dma((CHUNKS,)),
            dma((CHUNKS,)), dma((CHUNKS,)),
            dma((nr, CHUNKS)), dma((nr, CHUNKS)),
            dma((nb,)), dma((nb,)),
            dma((nr,)), dma((nr,)),
            dma((nb,)), dma((nb,)),
        ],
        compiler_params=pltpu.CompilerParams(
            collective_id=0, has_side_effects=True, vmem_limit_bytes=min(VMEM_MAX, need + (4 << 20))
        ),
        name="exchange",
    )(window, prev_pre, weight)


def local(nb, nr, grad_out, pre_act, prev_pre, weight, block_values, block_rows, block_cols):
    stripe_rows, width = grad_out.shape
    window = window_sums(block_rows, block_cols, grad_out, pre_act, block_values)
    window = window.reshape(SPANS, nr, stripe_rows // nr, width)
    return tuple(exchange(nb, nr, window, prev_pre, weight, stripe_rows * nb))


def solution(mesh):
    in_specs = (
        P("blk", None),
        P("blk", None),
        P(("blk", "rep"), None),
        P(),
        P(("blk", "rep"), None, None),
        P(("blk", "rep")),
        P(("blk", "rep")),
    )
    out_specs = (P(("blk", "rep"), None), P())
    body = functools.partial(local, mesh.shape["blk"], mesh.shape["rep"])
    return jax.shard_map(body, mesh=mesh, in_specs=in_specs, out_specs=out_specs, check_vma=False)
```

```python
import functools
import math

import jax
import jax.numpy as jnp
from jax import lax
from jax.experimental import pallas as pl
from jax.experimental.pallas import tpu as pltpu
from jax.sharding import PartitionSpec as P

HALO = 2
SPANS = 2 * HALO + 1
MESH = pl.DeviceIdType.MESH
VMEM_MAX = 67_043_328
CHUNKS = 16
GROUP = 4
STEP = 24


def window_kernel(rows_ref, cols_ref, grad_ref, pre_ref, values_ref, out_ref, masked, window, sem):
    step = pl.program_id(0)

    @pl.when(step == 0)
    def _():
        masked[...] = jnp.where(pre_ref[...] > 0, grad_ref[...], jnp.zeros_like(grad_ref[...])).reshape(masked.shape)

        @pl.loop(0, window.shape[0])
        def _(i):
            window[i] = jnp.zeros(window.shape[1:], window.dtype)

    count = values_ref.shape[0]

    @pl.loop(0, count // GROUP)
    def _(group):
        tiles = []
        for i in range(GROUP):
            k = group * GROUP + i
            tiles.append(
                lax.dot_general(
                    values_ref[k],
                    masked[rows_ref[step * count + k]],
                    (((0,), (0,)), ((), ())),
                    preferred_element_type=jnp.float32,
                )
            )
        for i in range(GROUP):
            col = cols_ref[step * count + group * GROUP + i]
            window[col] = window[col] + tiles[i]

    @pl.when(step == pl.num_programs(0) - 1)
    def _():
        copy = pltpu.make_async_copy(window, out_ref, sem)
        copy.start()
        copy.wait()


def window_sums(rows, cols, grad_out, pre_act, values):
    count, block, _ = values.shape
    stripe_rows, width = grad_out.shape
    stripe_blocks = stripe_rows // block
    whole = pl.BlockSpec((stripe_rows, width), lambda i, *_: (0, 0))
    return pl.pallas_call(
        window_kernel,
        out_shape=jax.ShapeDtypeStruct((SPANS * stripe_blocks, block, width), jnp.float32),
        grid_spec=pltpu.PrefetchScalarGridSpec(
            num_scalar_prefetch=2,
            grid=(count // STEP,),
            in_specs=[whole, whole, pl.BlockSpec((STEP, block, block), lambda i, *_: (i, 0, 0))],
            out_specs=pl.BlockSpec(memory_space=pl.ANY),
            scratch_shapes=[
                pltpu.VMEM((stripe_blocks, block, width), jnp.bfloat16),
                pltpu.VMEM((SPANS * stripe_blocks, block, width), jnp.float32),
                pltpu.SemaphoreType.DMA,
            ],
        ),
        compiler_params=pltpu.CompilerParams(vmem_limit_bytes=56 << 20),
        name="window_sums",
    )(rows, cols, grad_out, pre_act, values)


def exchange_kernel(
    nb, nr, scale,
    win, prev_ref, weight_ref, grad_in_ref, gw_ref,
    acc, core_in, z_in, y_in, x_in, dy, term, term_in, rep_in, total,
    s_load, s_core, r_core, s_z, r_z, s_y, r_y, s_x, r_x, s_t, r_t, s_r, r_r, s_g, r_g,
):
    b, r = lax.axis_index("blk"), lax.axis_index("rep")
    core, chip = b % 2, b // 2
    y, chips = chip % 2, nb // 2
    rows = dy.shape[0]
    size = rows // CHUNKS

    loads = [pltpu.make_async_copy(win.at[2 * i], acc.at[i], s_load.at[i]) for i in range(3)]
    for load in loads:
        load.start()

    barrier = pltpu.get_barrier_semaphore()
    for d in range(1, nb):
        pl.semaphore_signal(barrier, inc=1, device_id=((b + d) % nb, r), device_id_type=MESH)
    for e in range(1, nr):
        pl.semaphore_signal(barrier, inc=1, device_id=(b, (r + e) % nr), device_id_type=MESH)
    pl.semaphore_wait(barrier, nb - 1 + nr - 1)

    def remote(src, dst, send, recv, to_b, to_r):
        return pltpu.make_async_remote_copy(
            src_ref=src, dst_ref=dst, send_sem=send, recv_sem=recv,
            device_id=(to_b, to_r), device_id_type=MESH,
        )

    def part(j):
        return pl.ds(j * size, size)

    far, near = 2 * y, 2 - 2 * y
    core_to = chip * 2 + 1 - core
    z_to = ((chip + 4 * y - 2 + chips) % chips) * 2 + core
    y_to = (chip + 1 - 2 * y) * 2 + core

    def core_copy(i, j):
        return remote(
            win.at[2 * i + 1, :, part(j), :], core_in.at[i, :, part(j), :],
            s_core.at[i, j], r_core.at[i, j], core_to, r,
        )

    def z_copy(j):
        return remote(acc.at[far, :, part(j), :], z_in.at[:, part(j), :], s_z.at[j], r_z.at[j], z_to, r)

    def y_copy(j):
        return remote(acc.at[near, :, part(j), :], y_in.at[:, part(j), :], s_y.at[j], r_y.at[j], y_to, r)

    def x_copy(e, j):
        q = (r + e) % nr
        return remote(acc.at[1, q, part(j), :], x_in.at[e, part(j), :], s_x.at[e, j], r_x.at[e, j], b, q)

    for j in range(CHUNKS):
        for i in range(2):
            core_copy(i, j).start()
    for load in loads:
        load.wait()

    for j in range(CHUNKS):
        for i in range(2):
            core_copy(i, j).wait_recv()
            acc[1 + i - core, :, part(j), :] += core_in[i, :, part(j), :]
        z_copy(j).start()

    for step in range(CHUNKS + 5):
        if step < CHUNKS:
            j = step
            z_copy(j).wait_recv()
            acc[near, :, part(j), :] += z_in[:, part(j), :]
            y_copy(j).start()
        if 0 <= step - 2 < CHUNKS:
            j = step - 2
            y_copy(j).wait_recv()
            acc[1, :, part(j), :] += y_in[:, part(j), :]
            for e in range(1, nr):
                x_copy(e, j).start()
        if 0 <= step - 5 < CHUNKS:
            j = step - 5
            mine = acc[1, r, part(j), :]
            for e in range(1, nr):
                x_copy(e, j).wait_recv()
                mine = mine + x_in[e, part(j), :]
            dy[part(j), :] = mine.astype(jnp.bfloat16)

    prev = prev_ref[...]
    feats = jnp.maximum(prev, jnp.zeros_like(prev))
    product = lax.dot_general(feats, dy[...], (((0,), (0,)), ((), ())), preferred_element_type=jnp.float32)
    term[...] = product.reshape(term.shape)

    def term_copy(d):
        to = (b + d) % nb
        return remote(term.at[to], term_in.at[d], s_t.at[d], r_t.at[d], to, r)

    def rep_copy(e):
        return remote(rep_in.at[r], rep_in.at[r], s_r.at[e], r_r.at[e], b, (r + e) % nr)

    def total_copy(d):
        return remote(total.at[b], total.at[b], s_g.at[d], r_g.at[d], (b + d) % nb, r)

    for d in range(1, nb):
        term_copy(d).start()
    back = lax.dot_general(dy[...], weight_ref[...], (((1,), (1,)), ((), ())), preferred_element_type=jnp.float32)
    grad_in_ref[...] = jnp.where(prev > 0, back, jnp.zeros_like(back)).astype(jnp.bfloat16)
    own = term[b]
    for d in range(1, nb):
        term_copy(d).wait_recv()
        own = own + term_in[d]
    rep_in[r] = own
    for e in range(1, nr):
        rep_copy(e).start()
    for e in range(1, nr):
        rep_copy(e).wait_recv()
    full = rep_in[0]
    for e in range(1, nr):
        full = full + rep_in[e]
    total[b] = full * scale
    for d in range(1, nb):
        total_copy(d).start()
    for d in range(1, nb):
        total_copy(d).wait_recv()
    gw_ref[...] = total[...].reshape(gw_ref.shape)

    for j in range(CHUNKS):
        for i in range(2):
            core_copy(i, j).wait_send()
        z_copy(j).wait_send()
        y_copy(j).wait_send()
        for e in range(1, nr):
            x_copy(e, j).wait_send()
    for d in range(1, nb):
        term_copy(d).wait_send()
        total_copy(d).wait_send()
    for e in range(1, nr):
        rep_copy(e).wait_send()


def exchange(nb, nr, window, prev_pre, weight, nodes):
    rows, width = prev_pre.shape
    slab = (nr, rows, width)
    f32 = jnp.float32
    piece = (width // nb, width)
    dma = pltpu.SemaphoreType.DMA
    vmem = pl.BlockSpec(memory_space=pltpu.VMEM)
    return pl.pallas_call(
        functools.partial(exchange_kernel, nb, nr, 1.0 / math.sqrt(nodes)),
        out_shape=(
            jax.ShapeDtypeStruct((rows, width), jnp.bfloat16),
            jax.ShapeDtypeStruct((width, width), f32),
        ),
        in_specs=[pl.BlockSpec(memory_space=pl.ANY), vmem, vmem],
        out_specs=(vmem, vmem),
        scratch_shapes=[
            pltpu.VMEM((3,) + slab, f32),
            pltpu.VMEM((2,) + slab, f32),
            pltpu.VMEM(slab, f32),
            pltpu.VMEM(slab, f32),
            pltpu.VMEM(slab, f32),
            pltpu.VMEM((rows, width), jnp.bfloat16),
            pltpu.VMEM((nb,) + piece, f32),
            pltpu.VMEM((nb,) + piece, f32),
            pltpu.VMEM((nr,) + piece, f32),
            pltpu.VMEM((nb,) + piece, f32),
            dma((3,)),
            dma((2, CHUNKS)), dma((2, CHUNKS)),
            dma((CHUNKS,)), dma((CHUNKS,)),
            dma((CHUNKS,)), dma((CHUNKS,)),
            dma((nr, CHUNKS)), dma((nr, CHUNKS)),
            dma((nb,)), dma((nb,)),
            dma((nr,)), dma((nr,)),
            dma((nb,)), dma((nb,)),
        ],
        compiler_params=pltpu.CompilerParams(
            collective_id=0, has_side_effects=True, vmem_limit_bytes=VMEM_MAX
        ),
        name="exchange",
    )(window, prev_pre, weight)


def local(nb, nr, grad_out, pre_act, prev_pre, weight, block_values, block_rows, block_cols):
    stripe_rows, width = grad_out.shape
    window = window_sums(block_rows, block_cols, grad_out, pre_act, block_values)
    window = window.reshape(SPANS, nr, stripe_rows // nr, width)
    return tuple(exchange(nb, nr, window, prev_pre, weight, stripe_rows * nb))


def solution(mesh):
    in_specs = (
        P("blk", None),
        P("blk", None),
        P(("blk", "rep"), None),
        P(),
        P(("blk", "rep"), None, None),
        P(("blk", "rep")),
        P(("blk", "rep")),
    )
    out_specs = (P(("blk", "rep"), None), P())
    body = functools.partial(local, mesh.shape["blk"], mesh.shape["rep"])
    return jax.shard_map(body, mesh=mesh, in_specs=in_specs, out_specs=out_specs, check_vma=False)
```
